256 devices in a mesh: dp: 8 (over x, core), ctx: 32 (over z, y).
Axes of the slice: x: 4, y: 4, z: 8, core: 2. Of those that a mesh axis runs over, the one named last changes fastest.
Arguments:
- queries: bfloat16 [8, 8192, 2048], P('dp', 'ctx'), may hold values from -19 to 19
- raw_keys: bfloat16 [8, 8192, 2048], P('dp', 'ctx'), may hold values from -6 to 6
- raw_values: bfloat16 [8, 8192, 2048], P('dp', 'ctx'), may hold values from -6 to 6
- beacon_queries: bfloat16 [8, 64, 2048], P('dp', 'ctx'), may hold values from -19 to 19
- beacon_keys: bfloat16 [8, 64, 2048], P('dp', 'ctx'), may hold values from -6 to 6
- beacon_values: bfloat16 [8, 64, 2048], P('dp', 'ctx'), may hold values from -6 to 6
- upstream: bfloat16 [8, 8192, 2048], P('dp', 'ctx'), may hold values from -6 to 6
- beacon_upstream: bfloat16 [8, 64, 2048], P('dp', 'ctx'), may hold values from -6 to 6
- key_gain: float32 [2048], replicated, may hold values from 0.1 to 1.9
- window: int32 [8], P('dp'), may hold values from 64 to 256, as said below
Outputs:
- grad_queries: bfloat16 [8, 8192, 2048], P('dp', 'ctx')
- grad_keys: bfloat16 [8, 8192, 2048], P('dp', 'ctx')
- grad_values: bfloat16 [8, 8192, 2048], P('dp', 'ctx')
- grad_beacon_queries: bfloat16 [8, 64, 2048], P('dp', 'ctx')
- grad_beacon_keys: bfloat16 [8, 64, 2048], P('dp', 'ctx')
- grad_beacon_values: bfloat16 [8, 64, 2048], P('dp', 'ctx')
- grad_gain: float32 [2048], replicated
The draws below stay inside these ranges and needn't reach their ends.
Inputs may be any that keep to these rules, and one draw needn't show every extreme that they name: One prompt's window is exactly 256 and one is exactly 64.
All inputs are finite; a program needn't handle non-finite values.
Results may differ from the reference program's by a relative error of at most 0.017.
Values may be sent and summed in bfloat16 or wider, within the bound.
A program may use at most 192 MiB of HBM per device.

```python
import jax
import jax.numpy as jnp
from jax import lax

H = 16
DH = 128
INTERVAL = 128
S_DEV = 256
HD = 2048
PROMPTS = 8
L = 8192
NB = 64
N_CTX = 32


def beacon_draws(key):
    base = jax.random.fold_in(key, 31)
    key_query, key_key, key_beacon = jax.random.split(base, 3)
    queries = jax.random.truncated_normal(key_query, -6.0, 6.0, (PROMPTS, L, HD), jnp.float32)
    keys_raw = jax.random.truncated_normal(key_key, -6.0, 6.0, (PROMPTS, L, HD), jnp.float32)
    beacon_q = jax.random.truncated_normal(key_beacon, -6.0, 6.0, (PROMPTS, NB, HD), jnp.float32)
    return (queries.astype(jnp.bfloat16), keys_raw.astype(jnp.bfloat16), beacon_q.astype(jnp.bfloat16))


def draw_queries(key, part):
    return beacon_draws(key)[0]


def draw_raw_keys(key, part):
    return beacon_draws(key)[1]


def draw_beacon_queries(key, part):
    return beacon_draws(key)[2]


def draw_window(key, part):
    key_width, key_first, key_second = jax.random.split(jax.random.fold_in(key, 5), 3)
    widths = jax.random.randint(key_width, (PROMPTS,), S_DEV // 4, S_DEV + 1)
    first = jax.random.randint(key_first, (), 0, PROMPTS)
    second = (first + 1 + jax.random.randint(key_second, (), 0, PROMPTS - 1)) % PROMPTS
    widths = widths.at[second].set(S_DEV // 4).at[first].set(S_DEV)
    return widths.astype(jnp.int32)


def steps_of(rng, extent, shards, smallest, high):
    factor_of = 1.0
    for dim, shards_of in shards:
        draws = jax.random.uniform(jax.random.fold_in(jax.random.fold_in(rng, 6), dim), (shards_of,), jnp.float32, smallest / len(shards), high / len(shards))
        factor_of = factor_of * jnp.repeat(jnp.exp(draws), extent[dim] // shards_of).reshape((-1,) + (1,) * (len(extent) - 1 - dim))
    return factor_of


def centred(rng, dims, spread, limit, cuts=(), kind=jnp.bfloat16):
    result = spread * jax.random.normal(rng, dims, jnp.float32)
    if cuts:
        result = result * steps_of(rng, dims, cuts, -0.22, 0.18)
    return jnp.clip(result, -limit, limit).astype(kind)


def setup_inputs(seed: int = 0) -> dict:
    arg_keys = jax.random.split(jax.random.key(seed), 11)
    return {
        "queries": draw_queries(jax.random.fold_in(arg_keys[10], 71), 0),
        "raw_keys": draw_raw_keys(jax.random.fold_in(arg_keys[10], 71), 0),
        "raw_values": centred(arg_keys[2], (PROMPTS, L, HD), 1.0, 6.0, ((0, 8), (1, 32))),
        "beacon_queries": draw_beacon_queries(jax.random.fold_in(arg_keys[10], 71), 0),
        "beacon_keys": centred(arg_keys[4], (PROMPTS, NB, HD), 1.0, 6.0, ((0, 8), (1, 32))),
        "beacon_values": centred(arg_keys[5], (PROMPTS, NB, HD), 1.0, 6.0, ((0, 8), (1, 32))),
        "upstream": centred(arg_keys[6], (PROMPTS, L, HD), 1.0, 6.0, ((0, 8), (1, 32))),
        "beacon_upstream": centred(arg_keys[7], (PROMPTS, NB, HD), 1.0, 6.0, ((0, 8), (1, 32))),
        "key_gain": jnp.clip(1.0 + 0.18 * jax.random.normal(arg_keys[8], (HD,), jnp.float32), 0.1, 1.9),
        "window": draw_window(jax.random.fold_in(arg_keys[10], 71), 0),
    }


def slab_allowed(slab, width_here, slab_len, per_slab, beacon_count):
    position = slab * slab_len + jnp.arange(slab_len, dtype=jnp.int32)
    key_position = (slab - 1) * slab_len + jnp.arange(2 * slab_len, dtype=jnp.int32)
    column = jnp.arange(beacon_count, dtype=jnp.int32)
    own_beacon = slab * per_slab + jnp.arange(per_slab, dtype=jnp.int32)
    raw_raw = (key_position[None, :] <= position[:, None]) & (key_position[None, :] > position[:, None] - width_here) & (key_position[None, :] >= 0)
    raw_beacon = INTERVAL * (column[None, :] + 1) <= position[:, None] - width_here + 1
    beacon_raw = (key_position[None, :] >= INTERVAL * own_beacon[:, None]) & (key_position[None, :] < INTERVAL * (own_beacon[:, None] + 1))
    beacon_beacon = column[None, :] <= own_beacon[:, None]
    upper = jnp.concatenate([raw_raw, raw_beacon], axis=1)
    lower = jnp.concatenate([beacon_raw, beacon_beacon], axis=1)
    return jnp.concatenate([upper, lower], axis=0)


def attend(query_block, grad_block, key_block, value_block, allowed):
    scale = DH ** -0.5
    query_f = query_block.astype(jnp.float32).reshape(query_block.shape[0], H, DH)
    grad_f = grad_block.astype(jnp.float32).reshape(grad_block.shape[0], H, DH)
    key_f = key_block.astype(jnp.float32).reshape(key_block.shape[0], H, DH)
    value_f = value_block.astype(jnp.float32).reshape(value_block.shape[0], H, DH)
    scores = jnp.einsum('rhd,khd->hrk', query_f, key_f) * scale
    scores = jnp.where(allowed[None], scores, -jnp.inf)
    peak = jnp.max(scores, axis=-1, keepdims=True)
    expo = jnp.exp(scores - peak)
    total = jnp.sum(expo, axis=-1, keepdims=True)
    probs = expo / total
    probs_low = lax.optimization_barrier(probs.astype(jnp.bfloat16)).astype(jnp.float32)
    output = jnp.einsum('hrk,khd->rhd', probs_low, value_f)
    delta = jnp.sum(grad_f * output, axis=-1).T[:, :, None]
    dprob = jnp.einsum('rhd,khd->hrk', grad_f, value_f)
    dscore = probs * (dprob - delta)
    dscore_low = lax.optimization_barrier(dscore.astype(jnp.bfloat16)).astype(jnp.float32)
    dquery = jnp.einsum('hrk,khd->rhd', dscore_low, key_f) * scale
    dkey = jnp.einsum('hrk,rhd->khd', dscore_low, query_f) * scale
    dvalue = jnp.einsum('hrk,rhd->khd', probs_low, grad_f)
    return dquery.reshape(query_block.shape[0], HD), dkey.reshape(key_block.shape[0], HD), dvalue.reshape(key_block.shape[0], HD)


def reference(queries, raw_keys, raw_values, beacon_queries, beacon_keys, beacon_values, upstream, beacon_upstream, key_gain, window):
    per_slab = S_DEV // INTERVAL

    def one_prompt(packed):
        q_p, k_p, v_p, bq_p, bk_p, bv_p, g_p, bg_p, width_here = packed
        gained = (bk_p.astype(jnp.float32) * key_gain).astype(jnp.bfloat16)

        def one_slab(slab):
            start = slab * S_DEV
            prev_start = jnp.maximum(start - S_DEV, 0).astype(jnp.int32)
            bstart = (slab * per_slab).astype(jnp.int32)
            query_block = jnp.concatenate([lax.dynamic_slice_in_dim(q_p, start, S_DEV, 0), lax.dynamic_slice_in_dim(bq_p, bstart, per_slab, 0)], axis=0)
            grad_block = jnp.concatenate([lax.dynamic_slice_in_dim(g_p, start, S_DEV, 0), lax.dynamic_slice_in_dim(bg_p, bstart, per_slab, 0)], axis=0)
            key_block = jnp.concatenate([lax.dynamic_slice_in_dim(k_p, prev_start, S_DEV, 0), lax.dynamic_slice_in_dim(k_p, start, S_DEV, 0), gained], axis=0)
            value_block = jnp.concatenate([lax.dynamic_slice_in_dim(v_p, prev_start, S_DEV, 0), lax.dynamic_slice_in_dim(v_p, start, S_DEV, 0), bv_p], axis=0)
            allowed = slab_allowed(slab, width_here, S_DEV, per_slab, NB)
            return attend(query_block, grad_block, key_block, value_block, allowed)

        dq_all, dk_all, dv_all = lax.map(one_slab, jnp.arange(N_CTX, dtype=jnp.int32))
        pad = jnp.zeros((1, S_DEV, HD), jnp.float32)
        dq_raw = dq_all[:, :S_DEV].reshape(L, HD)
        dq_beacon = dq_all[:, S_DEV:].reshape(NB, HD)
        dk_raw = (dk_all[:, S_DEV:2 * S_DEV] + jnp.concatenate([dk_all[1:, :S_DEV], pad], axis=0)).reshape(L, HD)
        dv_raw = (dv_all[:, S_DEV:2 * S_DEV] + jnp.concatenate([dv_all[1:, :S_DEV], pad], axis=0)).reshape(L, HD)
        gained_grad = jnp.sum(dk_all[:, 2 * S_DEV:], axis=0)
        beacon_value_grad = jnp.sum(dv_all[:, 2 * S_DEV:], axis=0)
        gain_term = jnp.sum(bk_p.astype(jnp.float32) * gained_grad, axis=0)
        return (dq_raw.astype(jnp.bfloat16), dk_raw.astype(jnp.bfloat16), dv_raw.astype(jnp.bfloat16),
                dq_beacon.astype(jnp.bfloat16), (key_gain * gained_grad).astype(jnp.bfloat16),
                beacon_value_grad.astype(jnp.bfloat16), gain_term)

    results = lax.map(one_prompt, (queries, raw_keys, raw_values, beacon_queries, beacon_keys, beacon_values, upstream, beacon_upstream, window))
    return (results[0], results[1], results[2], results[3], results[4], results[5], jnp.sum(results[6], axis=0))
```

```python
from functools import partial
import math

import jax
import jax.numpy as jnp
from jax import lax
from jax.experimental import pallas as pl
from jax.experimental.pallas import tpu as pltpu
from jax.sharding import PartitionSpec as P

DH = 128
NY = 4
HALF = 128
ROWS = 144
WCOLS = 384
MESH = pl.DeviceIdType.MESH
NEG = -1e30
CONTRACT_LAST = (((1,), (1,)), ((), ()))
CONTRACT_FIRST = (((0,), (0,)), ((), ()))


def dot_t(a, b):
    return lax.dot_general(a, b, CONTRACT_LAST, preferred_element_type=jnp.float32)


def dot_f(a, b):
    return lax.dot_general(a, b, CONTRACT_FIRST, preferred_element_type=jnp.float32)


def dot_n(a, b):
    return jnp.dot(a, b, preferred_element_type=jnp.float32)


def kernel(
    ndp, nctx, heads, window,
    q_hbm, k_hbm, v_hbm, g_hbm, bkv, bqg, gain,
    dq_hbm, dk_hbm, dv_hbm, small, gain_out,
    q_s, k_s, v_s, g_s, dq_s, kv_prev, pg_s, pg_r, own_s, out_s,
    gath, kf, vf, bias_w, bias_b, rs_s, rs_r, zsum, ry_s, ry_r,
    gl, gd_r, gz_s, gz_r, gy_s, gy_r,
    in_sem, out_sem, kv_send, kv_recv, gath_send, gathy_recv, gathz_recv,
    pg_send, pg_recv, rs_send, rs_recv, ry_send, ry_recv,
    gd_send, gd_recv, gz_send, gz_recv, gy_send, gy_recv,
):
    nz = nctx // NY
    nb = 2 * nctx
    groups = heads // 4
    scale = DH ** (-0.5)
    dp = lax.axis_index("dp")
    ctx = lax.axis_index("ctx")
    z = ctx // NY
    y = ctx % NY
    after = (ctx + 1) % nctx
    before = (ctx + nctx - 1) % nctx

    def zpeer(j):
        return ((z + j) % nz) * NY + y

    def ypeer(j):
        return z * NY + (y + j) % NY

    def remote(src, dst, send, recv, to):
        return pltpu.make_async_remote_copy(
            src_ref=src, dst_ref=dst, send_sem=send, recv_sem=recv,
            device_id=to, device_id_type=MESH,
        )

    def drain(ref, sem):
        pltpu.make_async_copy(ref, ref, sem).wait()

    loads = [
        pltpu.make_async_copy(src, dst, in_sem.at[i])
        for i, (src, dst) in enumerate(
            ((q_hbm, q_s), (k_hbm, k_s), (v_hbm, v_s), (g_hbm, g_s))
        )
    ]
    for load in loads:
        load.start()
    own_block = pltpu.make_async_copy(bkv, gath.at[:, ctx], in_sem.at[4])
    own_block.start()

    barrier = pltpu.get_barrier_semaphore()
    pl.semaphore_signal(barrier, inc=1, device_id=(dp, after), device_id_type=MESH)
    pl.semaphore_signal(barrier, inc=1, device_id=(dp, before), device_id_type=MESH)

    @pl.loop(1, NY)
    def _(j):
        pl.semaphore_signal(barrier, inc=1, device_id=(dp, ypeer(j)), device_id_type=MESH)

    @pl.loop(1, nz)
    def _(j):
        pl.semaphore_signal(barrier, inc=1, device_id=(dp, zpeer(j)), device_id_type=MESH)

    @pl.loop(1, ndp)
    def _(j):
        pl.semaphore_signal(
            barrier, inc=1, device_id=((dp + j) % ndp, ctx), device_id_type=MESH
        )

    pl.semaphore_wait(barrier, 2 + NY - 1 + nz - 1 + ndp - 1)

    @pl.loop(1, NY)
    def _(j):
        remote(
            bkv, gath.at[:, ctx], gath_send.at[0], gathy_recv.at[0], (dp, ypeer(j))
        ).start()

    @pl.loop(0, heads)
    def _(h):
        cols = pl.ds(pl.multiple_of(h * DH, DH), DH)
        remote(
            k_hbm.at[:, cols], kv_prev.at[h, 0], kv_send.at[0], kv_recv.at[h], (dp, after)
        ).start()
        remote(
            v_hbm.at[:, cols], kv_prev.at[h, 1], kv_send.at[0], kv_recv.at[h], (dp, after)
        ).start()

    width = window[0]
    for k in range(2):
        row = lax.broadcasted_iota(jnp.int32, (ROWS, WCOLS), 0)
        col = lax.broadcasted_iota(jnp.int32, (ROWS, WCOLS), 1)
        key_position = (ctx - 1) * 2 * HALF + HALF * k + col
        raw = (
            (row < HALF)
            & (col <= 2 * HALF + row)
            & (col > 2 * HALF + row - width)
            & (key_position >= 0)
        )
        beacon = (row == HALF) & (col >= 2 * HALF)
        bias_w[k] = jnp.where(raw | beacon, 0.0, NEG)
        row = lax.broadcasted_iota(jnp.int32, (ROWS, nb), 0)
        col = lax.broadcasted_iota(jnp.int32, (ROWS, nb), 1)
        position = ctx * 2 * HALF + HALF * k + row
        raw = (row < HALF) & (HALF * (col + 1) <= position - width + 1)
        beacon = (row == HALF) & (col <= 2 * ctx + k)
        bias_b[k] = jnp.where(raw | beacon, 0.0, NEG)

    drain(gath.at[:, pl.ds(0, NY - 1)], gathy_recv.at[0])
    own_block.wait()
    for g in range(groups):
        @pl.loop(1, nz)
        def _(j):
            mine = pl.ds(z * NY, NY)
            remote(
                gath.at[g, mine], gath.at[g, mine], gath_send.at[1], gathz_recv.at[g],
                (dp, zpeer(j)),
            ).start()

    for load in loads:
        load.wait()

    first_row = lax.broadcasted_iota(jnp.int32, (16, DH), 0) == 0
    fold = scale * math.log2(math.e)

    @pl.loop(0, groups)
    def _(g):
        drain(gath.at[0, pl.ds(0, (nz - 1) * NY)], gathz_recv.at[g])
        block = gath[g].astype(jnp.float32)
        kf[...] = block[:, 0:8].reshape(nctx * 8, DH)
        vf[...] = block[:, 8:16].reshape(nctx * 8, DH)

        @pl.loop(0, 4)
        def _(hl):
            h = g * 4 + hl
            cols = pl.ds(pl.multiple_of(h * DH, DH), DH)
            raw_b = kf[pl.ds(hl, nb, stride=4), :]
            gained = (raw_b * gain[pl.ds(h, 1), :]).astype(jnp.bfloat16)
            value_b = vf[pl.ds(hl, nb, stride=4), :].astype(jnp.bfloat16)
            drain(kv_prev.at[h], kv_recv.at[h])
            win_k = []
            win_v = []
            for k in range(2):
                win_k.append(
                    jnp.concatenate(
                        [kv_prev[h, 0, HALF * k :], k_s[0 : HALF * (k + 1), cols]], axis=0
                    )
                )
                win_v.append(
                    jnp.concatenate(
                        [kv_prev[h, 1, HALF * k :], v_s[0 : HALF * (k + 1), cols]], axis=0
                    )
                )
            dk_w, dv_w, dk_b, dv_b = [], [], [], []
            for k in range(2):
                extra_q = jnp.where(first_row, bqg[k, pl.ds(h, 1), :], 0.0)
                extra_g = jnp.where(first_row, bqg[2 + k, pl.ds(h, 1), :], 0.0)
                rows = slice(HALF * k, HALF * (k + 1))
                q = jnp.concatenate([q_s[rows, cols], extra_q.astype(jnp.bfloat16)], axis=0)
                up = jnp.concatenate([g_s[rows, cols], extra_g.astype(jnp.bfloat16)], axis=0)
                s_w = dot_t(q, win_k[k]) * fold + bias_w[k]
                s_b = dot_t(q, gained) * fold + bias_b[k]
                peak = jnp.maximum(
                    jnp.max(s_w, axis=1, keepdims=True), jnp.max(s_b, axis=1, keepdims=True)
                )
                e_w = jnp.exp2(s_w - peak)
                e_b = jnp.exp2(s_b - peak)
                total = jnp.sum(e_w, axis=1, keepdims=True) + jnp.sum(
                    e_b, axis=1, keepdims=True
                )
                inverse = 1.0 / total
                p_w = e_w * inverse
                p_b = e_b * inverse
                low_w = p_w.astype(jnp.bfloat16)
                low_b = p_b.astype(jnp.bfloat16)
                dp_w = dot_t(up, win_v[k])
                dp_b = dot_t(up, value_b)
                delta = jnp.sum(
                    low_w.astype(jnp.float32) * dp_w, axis=1, keepdims=True
                ) + jnp.sum(low_b.astype(jnp.float32) * dp_b, axis=1, keepdims=True)
                ds_w = (p_w * (dp_w - delta)).astype(jnp.bfloat16)
                ds_b = (p_b * (dp_b - delta)).astype(jnp.bfloat16)
                dk_w.append(dot_f(ds_w, q))
                dv_w.append(dot_f(low_w, up))
                dk_b.append(dot_f(ds_b, q))
                dv_b.append(dot_f(low_b, up))
                dq = (dot_n(ds_w, win_k[k]) + dot_n(ds_b, gained)) * scale
                dq_s[rows, cols] = dq[0:HALF].astype(jnp.bfloat16)
                gz_s[1 + k, pl.ds(h, 1), :] = dq[HALF : HALF + 1]
            for i, (t, c) in enumerate(((dk_w, scale), (dv_w, 1.0))):
                pg_s[h, i, 0:HALF] = (t[0][0:HALF] * c).astype(jnp.bfloat16)
                pg_s[h, i, HALF:] = (
                    (t[0][HALF : 2 * HALF] + t[1][0:HALF]) * c
                ).astype(jnp.bfloat16)
            part_k = (dk_b[0] + dk_b[1]) * scale
            part_v = dv_b[0] + dv_b[1]
            rs_s[h] = jnp.concatenate(
                [part_k.reshape(nz, 8, DH), part_v.reshape(nz, 8, DH)], axis=1
            ).astype(jnp.bfloat16)
            gl[pl.ds(h, 1), :] = jnp.sum(raw_b * part_k, axis=0, keepdims=True)
            for i, (t, c) in enumerate(((dk_w, scale), (dv_w, 1.0))):
                own_s[h, i, 0:HALF] = (t[0][2 * HALF :] + t[1][HALF : 2 * HALF]) * c
                own_s[h, i, HALF:] = t[1][2 * HALF :] * c
            remote(
                pg_s.at[h], pg_r.at[h], pg_send.at[0], pg_recv.at[h], (dp, before)
            ).start()

            @pl.loop(1, nz)
            def _(j):
                remote(
                    rs_s.at[h, (z + j) % nz], rs_r.at[h, z], rs_send.at[0], rs_recv.at[0],
                    (dp, zpeer(j)),
                ).start()

    store_q = pltpu.make_async_copy(dq_s, dq_hbm, out_sem.at[0])
    store_q.start()

    @pl.loop(1, ndp)
    def _(j):
        remote(
            gl, gd_r.at[dp], gd_send.at[0], gd_recv.at[0], ((dp + j) % ndp, ctx)
        ).start()

    gd_r[dp] = gl[...]
    rs_r[:, z] = rs_s[:, z]

    drain(rs_r.at[:, pl.ds(0, nz - 1)], rs_recv.at[0])
    zsum[...] = jnp.sum(rs_r[...].astype(jnp.float32), axis=1).reshape(heads * 16, DH)
    for t in range(NY):
        for kv in range(2):
            for k in range(2):
                ry_s[t, 2 * kv + k] = zsum[
                    pl.ds(kv * 8 + 2 * t + k, heads, stride=16), :
                ].astype(jnp.bfloat16)

    @pl.loop(1, NY)
    def _(j):
        remote(
            ry_s.at[(y + j) % NY], ry_r.at[y], ry_send.at[0], ry_recv.at[0], (dp, ypeer(j))
        ).start()

    ry_r[y] = ry_s[y]

    drain(gd_r.at[pl.ds(0, ndp - 1)], gd_recv.at[0])
    gz_s[0] = jnp.sum(gd_r[...], axis=0)
    gz_r[z] = gz_s[0]

    @pl.loop(1, nz)
    def _(j):
        remote(
            gz_s.at[0], gz_r.at[z], gz_send.at[0], gz_recv.at[0], (dp, zpeer(j))
        ).start()

    @pl.loop(0, heads)
    def _(h):
        cols = pl.ds(pl.multiple_of(h * DH, DH), DH)
        drain(pg_r.at[h], pg_recv.at[h])
        total = own_s[h] + pg_r[h].astype(jnp.float32)
        out_s[0, :, cols] = total[0].astype(jnp.bfloat16)
        out_s[1, :, cols] = total[1].astype(jnp.bfloat16)
        pltpu.make_async_copy(
            out_s.at[0, :, cols], dk_hbm.at[:, cols], out_sem.at[1]
        ).start()
        pltpu.make_async_copy(
            out_s.at[1, :, cols], dv_hbm.at[:, cols], out_sem.at[2]
        ).start()

    drain(gz_r.at[pl.ds(0, nz - 1)], gz_recv.at[0])
    gy_s[...] = jnp.sum(gz_r[...], axis=0)
    gy_r[y] = gy_s[...]

    @pl.loop(1, NY)
    def _(j):
        remote(gy_s, gy_r.at[y], gy_send.at[0], gy_recv.at[0], (dp, ypeer(j))).start()

    drain(ry_r.at[pl.ds(0, NY - 1)], ry_recv.at[0])
    own = jnp.sum(ry_r[...].astype(jnp.float32), axis=0)
    for k in range(2):
        small[k] = gz_s[1 + k].astype(jnp.bfloat16)
        small[2 + k] = (own[k] * gain[...]).astype(jnp.bfloat16)
        small[4 + k] = own[2 + k].astype(jnp.bfloat16)
    drain(gy_r.at[pl.ds(0, NY - 1)], gy_recv.at[0])
    gain_out[...] = jnp.sum(gy_r[...], axis=0)

    drain(gath.at[:, pl.ds(0, NY - 1)], gath_send.at[0])
    drain(gath.at[:, pl.ds(0, (nz - 1) * NY)], gath_send.at[1])
    drain(kv_prev, kv_send.at[0])
    drain(pg_s, pg_send.at[0])
    drain(rs_s.at[:, pl.ds(0, nz - 1)], rs_send.at[0])
    drain(ry_s.at[pl.ds(0, NY - 1)], ry_send.at[0])
    drain(gd_r.at[pl.ds(0, ndp - 1)], gd_send.at[0])
    drain(gz_r.at[pl.ds(0, nz - 1)], gz_send.at[0])
    drain(gy_r.at[pl.ds(0, NY - 1)], gy_send.at[0])
    store_q.wait()
    drain(dk_hbm, out_sem.at[1])
    drain(dv_hbm, out_sem.at[2])


def on_device(
    queries, raw_keys, raw_values, beacon_queries, beacon_keys, beacon_values,
    upstream, beacon_upstream, key_gain, window,
):
    ndp = lax.axis_size("dp")
    nctx = lax.axis_size("ctx")
    nz = nctx // NY
    nb = 2 * nctx
    slab = queries.shape[1]
    hd = queries.shape[2]
    heads = hd // DH
    groups = heads // 4
    bf16, f32 = jnp.bfloat16, jnp.float32

    def grouped(block):
        return block.reshape(2, groups, 4, DH).transpose(1, 0, 2, 3).reshape(groups, 8, DH)

    bkv = jnp.concatenate([grouped(beacon_keys), grouped(beacon_values)], axis=1)
    bqg = jnp.concatenate([beacon_queries[0], beacon_upstream[0]], axis=0)
    bqg = bqg.astype(f32).reshape(4, heads, DH)
    vmem = pl.BlockSpec(memory_space=pltpu.VMEM)
    anyspace = pl.BlockSpec(memory_space=pl.ANY)
    dma = pltpu.SemaphoreType.DMA
    big = jax.ShapeDtypeStruct((slab, hd), bf16)
    outs = pl.pallas_call(
        partial(kernel, ndp, nctx, heads),
        out_shape=(
            big, big, big,
            jax.ShapeDtypeStruct((6, heads, DH), bf16),
            jax.ShapeDtypeStruct((heads, DH), f32),
        ),
        in_specs=[pl.BlockSpec(memory_space=pltpu.SMEM)] + [anyspace] * 4 + [vmem] * 3,
        out_specs=(anyspace, anyspace, anyspace, vmem, vmem),
        scratch_shapes=[
            pltpu.VMEM((slab, hd), bf16),
            pltpu.VMEM((slab, hd), bf16),
            pltpu.VMEM((slab, hd), bf16),
            pltpu.VMEM((slab, hd), bf16),
            pltpu.VMEM((slab, hd), bf16),
            pltpu.VMEM((heads, 2, slab, DH), bf16),
            pltpu.VMEM((heads, 2, slab, DH), bf16),
            pltpu.VMEM((heads, 2, slab, DH), bf16),
            pltpu.VMEM((heads, 2, slab, DH), f32),
            pltpu.VMEM((2, slab, hd), bf16),
            pltpu.VMEM((groups, nctx, 16, DH), bf16),
            pltpu.VMEM((nctx * 8, DH), f32),
            pltpu.VMEM((nctx * 8, DH), f32),
            pltpu.VMEM((2, ROWS, WCOLS), f32),
            pltpu.VMEM((2, ROWS, nb), f32),
            pltpu.VMEM((heads, nz, 16, DH), bf16),
            pltpu.VMEM((heads, nz, 16, DH), bf16),
            pltpu.VMEM((heads * 16, DH), f32),
            pltpu.VMEM((NY, 4, heads, DH), bf16),
            pltpu.VMEM((NY, 4, heads, DH), bf16),
            pltpu.VMEM((heads, DH), f32),
            pltpu.VMEM((ndp, heads, DH), f32),
            pltpu.VMEM((3, heads, DH), f32),
            pltpu.VMEM((nz, heads, DH), f32),
            pltpu.VMEM((heads, DH), f32),
            pltpu.VMEM((NY, heads, DH), f32),
            dma((5,)), dma((3,)), dma((1,)), dma((heads,)), dma((2,)), dma((1,)),
            dma((groups,)), dma((1,)), dma((heads,)), dma((1,)), dma((1,)), dma((1,)),
            dma((1,)), dma((1,)), dma((1,)), dma((1,)), dma((1,)), dma((1,)), dma((1,)),
        ],
        compiler_params=pltpu.CompilerParams(
            collective_id=0, has_side_effects=True, vmem_limit_bytes=56 * 1024 * 1024
        ),
        name="beacon_backward",
    )(
        window, queries[0], raw_keys[0], raw_values[0], upstream[0], bkv, bqg,
        key_gain.reshape(heads, DH),
    )
    dq, dk, dv, small, gain = outs
    small = small.reshape(3, 1, 2, hd)
    return dq[None], dk[None], dv[None], small[0], small[1], small[2], gain.reshape(hd)


def solution(mesh):
    slabs = P("dp", "ctx", None)
    return jax.shard_map(
        on_device,
        mesh=mesh,
        in_specs=(slabs,) * 8 + (P(), P("dp")),
        out_specs=(slabs,) * 6 + (P(),),
        check_vma=False,
    )
```

```python
from functools import partial
import math

import jax
import jax.numpy as jnp
from jax import lax
from jax.experimental import pallas as pl
from jax.experimental.pallas import tpu as pltpu
from jax.sharding import PartitionSpec as P

DH = 128
NY = 4
HALF = 128
ROWS = 144
AHEAD = 2
LAST = 3
WCOLS = 384
MESH = pl.DeviceIdType.MESH
NEG = -1e30
CONTRACT_LAST = (((1,), (1,)), ((), ()))
CONTRACT_FIRST = (((0,), (0,)), ((), ()))


def dot_t(a, b):
    return lax.dot_general(a, b, CONTRACT_LAST, preferred_element_type=jnp.float32)


def dot_f(a, b):
    return lax.dot_general(a, b, CONTRACT_FIRST, preferred_element_type=jnp.float32)


def dot_n(a, b):
    return jnp.dot(a, b, preferred_element_type=jnp.float32)


def kernel(
    ndp, nctx, heads, window,
    q_hbm, k_hbm, v_hbm, g_hbm, bkv, bqg, gain,
    dq_out, dk_out, dv_out, dbq, dbk, dbv, gain_out,
    q_s, k_s, v_s, g_s, kv_prev, pg_s, pg_r, own_s,
    gath, kf, vf, bias_w, bias_b, rs_s, rs_r, zsum, ry_s, ry_r,
    gl, gd_r, gz_s, gz_r, gy_s, gy_r,
    in_sem, kv_send, kv_recv, gath_send, gathy_recv, gathz_send, gathz_recv,
    pg_send, pg_recv, rs_send, rs_recv, ry_send, ry_recv,
    gd_send, gd_recv, gz_send, gz_recv, gy_send, gy_recv,
):
    nz = nctx // NY
    nb = 2 * nctx
    groups = heads // 4
    scale = DH ** (-0.5)
    dp = lax.axis_index("dp")
    ctx = lax.axis_index("ctx")
    z = ctx // NY
    y = ctx % NY
    after = (ctx + 1) % nctx
    before = (ctx + nctx - 1) % nctx

    def zpeer(j):
        return ((z + j) % nz) * NY + y

    def ypeer(j):
        return z * NY + (y + j) % NY

    def remote(src, dst, send, recv, to):
        return pltpu.make_async_remote_copy(
            src_ref=src, dst_ref=dst, send_sem=send, recv_sem=recv,
            device_id=to, device_id_type=MESH,
        )

    def drain(ref, sem):
        pltpu.make_async_copy(ref, ref, sem).wait()

    loads = [
        pltpu.make_async_copy(src, dst, in_sem.at[i])
        for i, (src, dst) in enumerate(
            ((q_hbm, q_s), (k_hbm, k_s), (v_hbm, v_s), (g_hbm, g_s))
        )
    ]
    for load in loads:
        load.start()
    own_block = pltpu.make_async_copy(bkv, gath.at[:, ctx], in_sem.at[4])
    own_block.start()

    barrier = pltpu.get_barrier_semaphore()
    pl.semaphore_signal(barrier, inc=1, device_id=(dp, after), device_id_type=MESH)
    pl.semaphore_signal(barrier, inc=1, device_id=(dp, before), device_id_type=MESH)

    @pl.loop(1, NY)
    def _(j):
        pl.semaphore_signal(barrier, inc=1, device_id=(dp, ypeer(j)), device_id_type=MESH)

    @pl.loop(1, nz)
    def _(j):
        pl.semaphore_signal(barrier, inc=1, device_id=(dp, zpeer(j)), device_id_type=MESH)

    @pl.loop(1, ndp)
    def _(j):
        pl.semaphore_signal(
            barrier, inc=1, device_id=((dp + j) % ndp, ctx), device_id_type=MESH
        )

    pl.semaphore_wait(barrier, 2 + NY - 1 + nz - 1 + ndp - 1)

    @pl.loop(1, NY)
    def _(j):
        remote(
            bkv, gath.at[:, ctx], gath_send.at[0], gathy_recv.at[0], (dp, ypeer(j))
        ).start()

    def send_kv(h):
        cols = pl.ds(pl.multiple_of(h * DH, DH), DH)
        for i, source in enumerate((k_hbm, v_hbm)):
            remote(
                source.at[:, cols], kv_prev.at[h, i], kv_send.at[0], kv_recv.at[h],
                (dp, after),
            ).start()

    @pl.loop(0, AHEAD)
    def _(h):
        send_kv(h)

    width = window[0]
    for k in range(2):
        row = lax.broadcasted_iota(jnp.int32, (ROWS, WCOLS), 0)
        col = lax.broadcasted_iota(jnp.int32, (ROWS, WCOLS), 1)
        key_position = (ctx - 1) * 2 * HALF + HALF * k + col
        raw = (
            (row < HALF)
            & (col <= 2 * HALF + row)
            & (col > 2 * HALF + row - width)
            & (key_position >= 0)
        )
        beacon = (row == HALF) & (col >= 2 * HALF)
        bias_w[k] = jnp.where(raw | beacon, 0.0, NEG)
        row = lax.broadcasted_iota(jnp.int32, (ROWS, nb), 0)
        col = lax.broadcasted_iota(jnp.int32, (ROWS, nb), 1)
        position = ctx * 2 * HALF + HALF * k + row
        raw = (row < HALF) & (HALF * (col + 1) <= position - width + 1)
        beacon = (row == HALF) & (col <= 2 * ctx + k)
        bias_b[k] = jnp.where(raw | beacon, 0.0, NEG)

    drain(gath.at[:, pl.ds(0, NY - 1)], gathy_recv.at[0])
    own_block.wait()

    def spread(g):
        @pl.loop(z + 1, nz)
        def _(t):
            mine = pl.ds(z * NY, NY)
            remote(
                gath.at[g, mine], gath.at[g, mine], gathz_send.at[t], gathz_recv.at[g, z],
                (dp, t * NY + y),
            ).start()

    spread(0)

    @pl.loop(z + 1, nz)
    def _(t):
        gath[:, pl.ds(t * NY, NY)] = jnp.zeros((groups, NY, 16, DH), jnp.bfloat16)

    @pl.loop(0, z)
    def _(t):
        rs_r[:, t] = jnp.zeros((heads, 16, DH), jnp.bfloat16)


    for load in loads:
        load.wait()

    first_row = lax.broadcasted_iota(jnp.int32, (16, DH), 0) == 0
    fold = scale * math.log2(math.e)

    @pl.loop(0, groups)
    def _(g):
        @pl.loop(0, z)
        def _(t):
            drain(gath.at[g, pl.ds(t * NY, NY)], gathz_recv.at[g, t])

        @pl.when(g + 1 < groups)
        def _():
            spread(g + 1)

        block = gath[g].astype(jnp.float32)
        kf[...] = block[:, 0:8].reshape(nctx * 8, DH)
        vf[...] = block[:, 8:16].reshape(nctx * 8, DH)

        @pl.loop(0, 4)
        def _(hl):
            h = g * 4 + hl
            cols = pl.ds(pl.multiple_of(h * DH, DH), DH)
            raw_b = kf[pl.ds(hl, nb, stride=4), :]
            gained = (raw_b * gain[pl.ds(h, 1), :]).astype(jnp.bfloat16)
            value_b = vf[pl.ds(hl, nb, stride=4), :].astype(jnp.bfloat16)
            drain(kv_prev.at[h], kv_recv.at[h])

            @pl.when(h + AHEAD < heads)
            def _():
                send_kv(h + AHEAD)

            win_k = []
            win_v = []
            for k in range(2):
                win_k.append(
                    jnp.concatenate(
                        [kv_prev[h, 0, HALF * k :], k_s[0 : HALF * (k + 1), cols]], axis=0
                    )
                )
                win_v.append(
                    jnp.concatenate(
                        [kv_prev[h, 1, HALF * k :], v_s[0 : HALF * (k + 1), cols]], axis=0
                    )
                )
            dk_w, dv_w, dk_b, dv_b = [], [], [], []
            for k in range(2):
                extra_q = jnp.where(first_row, bqg[k, pl.ds(h, 1), :], 0.0)
                extra_g = jnp.where(first_row, bqg[2 + k, pl.ds(h, 1), :], 0.0)
                rows = slice(HALF * k, HALF * (k + 1))
                q = jnp.concatenate([q_s[rows, cols], extra_q.astype(jnp.bfloat16)], axis=0)
                up = jnp.concatenate([g_s[rows, cols], extra_g.astype(jnp.bfloat16)], axis=0)
                s_w = dot_t(q, win_k[k]) * fold + bias_w[k]
                s_b = dot_t(q, gained) * fold + bias_b[k]
                peak = jnp.maximum(
                    jnp.max(s_w, axis=1, keepdims=True), jnp.max(s_b, axis=1, keepdims=True)
                )
                e_w = jnp.exp2(s_w - peak)
                e_b = jnp.exp2(s_b - peak)
                total = jnp.sum(e_w, axis=1, keepdims=True) + jnp.sum(
                    e_b, axis=1, keepdims=True
                )
                inverse = 1.0 / total
                p_w = e_w * inverse
                p_b = e_b * inverse
                low_w = p_w.astype(jnp.bfloat16)
                low_b = p_b.astype(jnp.bfloat16)
                dp_w = dot_t(up, win_v[k])
                dp_b = dot_t(up, value_b)
                delta = jnp.sum(
                    low_w.astype(jnp.float32) * dp_w, axis=1, keepdims=True
                ) + jnp.sum(low_b.astype(jnp.float32) * dp_b, axis=1, keepdims=True)
                ds_w = (p_w * (dp_w - delta)).astype(jnp.bfloat16)
                ds_b = (p_b * (dp_b - delta)).astype(jnp.bfloat16)
                dk_w.append(dot_f(ds_w, q))
                dv_w.append(dot_f(low_w, up))
                dk_b.append(dot_f(ds_b, q))
                dv_b.append(dot_f(low_b, up))
                dq = (dot_n(ds_w, win_k[k]) + dot_n(ds_b, gained)) * scale
                dq_out[rows, cols] = dq[0:HALF].astype(jnp.bfloat16)
                gz_s[1 + k, pl.ds(h, 1), :] = dq[HALF : HALF + 1]
            for i, (t, c) in enumerate(((dk_w, scale), (dv_w, 1.0))):
                pg_s[h, i, 0:HALF] = (t[0][0:HALF] * c).astype(jnp.bfloat16)
                pg_s[h, i, HALF:] = (
                    (t[0][HALF : 2 * HALF] + t[1][0:HALF]) * c
                ).astype(jnp.bfloat16)
            part_k = (dk_b[0] + dk_b[1]) * scale
            part_v = dv_b[0] + dv_b[1]
            rs_s[h] = jnp.concatenate(
                [part_k.reshape(nz, 8, DH), part_v.reshape(nz, 8, DH)], axis=1
            ).astype(jnp.bfloat16)
            gl[pl.ds(h, 1), :] = jnp.sum(raw_b * part_k, axis=0, keepdims=True)
            for i, (t, c) in enumerate(((dk_w, scale), (dv_w, 1.0))):
                own_s[h, i, 0:HALF] = (t[0][2 * HALF :] + t[1][HALF : 2 * HALF]) * c
                own_s[h, i, HALF:] = t[1][2 * HALF :] * c
            remote(
                pg_s.at[h], pg_r.at[h], pg_send.at[0], pg_recv.at[h], (dp, before)
            ).start()

            @pl.loop(0, z)
            def _(t):
                remote(
                    rs_s.at[h, t], rs_r.at[h, z], rs_send.at[t], rs_recv.at[z],
                    (dp, t * NY + y),
                ).start()

    @pl.loop(1, ndp)
    def _(j):
        remote(
            gl, gd_r.at[dp], gd_send.at[0], gd_recv.at[0], ((dp + j) % ndp, ctx)
        ).start()

    gd_r[dp] = gl[...]
    rs_r[:, z] = rs_s[:, z]

    drain(gd_r.at[pl.ds(0, ndp - 1)], gd_recv.at[0])
    gz_s[0] = jnp.sum(gd_r[...], axis=0)
    gz_r[z] = gz_s[0]

    @pl.loop(1, nz)
    def _(j):
        remote(
            gz_s.at[0], gz_r.at[z], gz_send.at[0], gz_recv.at[0], (dp, zpeer(j))
        ).start()

    @pl.loop(z + 1, nz)
    def _(t):
        drain(rs_r.at[:, t], rs_recv.at[t])

    zsum[...] = jnp.sum(rs_r[...].astype(jnp.float32), axis=1).reshape(heads * 16, DH)
    for t in range(NY):
        for kv in range(2):
            for k in range(2):
                ry_s[t, 2 * kv + k] = zsum[
                    pl.ds(kv * 8 + 2 * t + k, heads, stride=16), :
                ].astype(jnp.bfloat16)

    @pl.loop(1, NY)
    def _(j):
        remote(
            ry_s.at[(y + j) % NY], ry_r.at[y], ry_send.at[0], ry_recv.at[0], (dp, ypeer(j))
        ).start()

    ry_r[y] = ry_s[y]

    def finish(h):
        cols = pl.ds(pl.multiple_of(h * DH, DH), DH)
        drain(pg_r.at[h], pg_recv.at[h])
        total = own_s[h] + pg_r[h].astype(jnp.float32)
        dk_out[:, cols] = total[0].astype(jnp.bfloat16)
        dv_out[:, cols] = total[1].astype(jnp.bfloat16)

    @pl.loop(0, heads - LAST)
    def _(h):
        finish(h)

    drain(gz_r.at[pl.ds(0, nz - 1)], gz_recv.at[0])
    gy_s[...] = jnp.sum(gz_r[...], axis=0)
    gy_r[y] = gy_s[...]

    @pl.loop(1, NY)
    def _(j):
        remote(gy_s, gy_r.at[y], gy_send.at[0], gy_recv.at[0], (dp, ypeer(j))).start()

    @pl.loop(heads - LAST, heads)
    def _(h):
        finish(h)

    drain(ry_r.at[pl.ds(0, NY - 1)], ry_recv.at[0])
    own = jnp.sum(ry_r[...].astype(jnp.float32), axis=0)
    for h in range(heads):
        cols = slice(h * DH, (h + 1) * DH)
        scaled = gain[h : h + 1]
        rows_q = [gz_s[1 + k, h : h + 1] for k in range(2)]
        rows_k = [own[k, h : h + 1] * scaled for k in range(2)]
        rows_v = [own[2 + k, h : h + 1] for k in range(2)]
        dbq[:, cols] = jnp.concatenate(rows_q, axis=0).astype(jnp.bfloat16)
        dbk[:, cols] = jnp.concatenate(rows_k, axis=0).astype(jnp.bfloat16)
        dbv[:, cols] = jnp.concatenate(rows_v, axis=0).astype(jnp.bfloat16)
    drain(gy_r.at[pl.ds(0, NY - 1)], gy_recv.at[0])
    gain_out[...] = jnp.sum(gy_r[...], axis=0)

    drain(gath.at[:, pl.ds(0, NY - 1)], gath_send.at[0])

    @pl.loop(z + 1, nz)
    def _(t):
        drain(gath.at[:, pl.ds(0, NY)], gathz_send.at[t])

    drain(kv_prev, kv_send.at[0])
    drain(pg_s, pg_send.at[0])

    @pl.loop(0, z)
    def _(t):
        drain(rs_s.at[:, t], rs_send.at[t])

    drain(ry_s.at[pl.ds(0, NY - 1)], ry_send.at[0])
    drain(gd_r.at[pl.ds(0, ndp - 1)], gd_send.at[0])
    drain(gz_r.at[pl.ds(0, nz - 1)], gz_send.at[0])
    drain(gy_r.at[pl.ds(0, NY - 1)], gy_send.at[0])


def on_device(
    queries, raw_keys, raw_values, beacon_queries, beacon_keys, beacon_values,
    upstream, beacon_upstream, key_gain, window,
):
    ndp = lax.axis_size("dp")
    nctx = lax.axis_size("ctx")
    nz = nctx // NY
    nb = 2 * nctx
    slab = queries.shape[1]
    hd = queries.shape[2]
    heads = hd // DH
    groups = heads // 4
    bf16, f32 = jnp.bfloat16, jnp.float32

    def grouped(block):
        return block.reshape(2, groups, 4, DH).transpose(1, 0, 2, 3).reshape(groups, 8, DH)

    bkv = jnp.concatenate([grouped(beacon_keys), grouped(beacon_values)], axis=1)
    bqg = jnp.concatenate([beacon_queries[0], beacon_upstream[0]], axis=0)
    bqg = bqg.astype(f32).reshape(4, heads, DH)
    vmem = pl.BlockSpec(memory_space=pltpu.VMEM)
    anyspace = pl.BlockSpec(memory_space=pl.ANY)
    dma = pltpu.SemaphoreType.DMA
    few = jax.ShapeDtypeStruct((2, hd), bf16)
    big = pltpu.VMEM((slab, hd), bf16)
    outs = pl.pallas_call(
        partial(kernel, ndp, nctx, heads),
        out_shape=(
            big, big, big,
            few, few, few,
            jax.ShapeDtypeStruct((heads, DH), f32),
        ),
        in_specs=[pl.BlockSpec(memory_space=pltpu.SMEM)] + [anyspace] * 4 + [vmem] * 3,
        out_specs=(vmem,) * 7,
        scratch_shapes=[
            pltpu.VMEM((slab, hd), bf16),
            pltpu.VMEM((slab, hd), bf16),
            pltpu.VMEM((slab, hd), bf16),
            pltpu.VMEM((slab, hd), bf16),
            pltpu.VMEM((heads, 2, slab, DH), bf16),
            pltpu.VMEM((heads, 2, slab, DH), bf16),
            pltpu.VMEM((heads, 2, slab, DH), bf16),
            pltpu.VMEM((heads, 2, slab, DH), f32),
            pltpu.VMEM((groups, nctx, 16, DH), bf16),
            pltpu.VMEM((nctx * 8, DH), f32),
            pltpu.VMEM((nctx * 8, DH), f32),
            pltpu.VMEM((2, ROWS, WCOLS), f32),
            pltpu.VMEM((2, ROWS, nb), f32),
            pltpu.VMEM((heads, nz, 16, DH), bf16),
            pltpu.VMEM((heads, nz, 16, DH), bf16),
            pltpu.VMEM((heads * 16, DH), f32),
            pltpu.VMEM((NY, 4, heads, DH), bf16),
            pltpu.VMEM((NY, 4, heads, DH), bf16),
            pltpu.VMEM((heads, DH), f32),
            pltpu.VMEM((ndp, heads, DH), f32),
            pltpu.VMEM((3, heads, DH), f32),
            pltpu.VMEM((nz, heads, DH), f32),
            pltpu.VMEM((heads, DH), f32),
            pltpu.VMEM((NY, heads, DH), f32),
            dma((5,)), dma((1,)), dma((heads,)), dma((1,)), dma((1,)),
            dma((nz,)), dma((groups, nz)), dma((1,)), dma((heads,)),
            dma((nz,)), dma((nz,)), dma((1,)), dma((1,)),
            dma((1,)), dma((1,)), dma((1,)), dma((1,)), dma((1,)), dma((1,)),
        ],
        compiler_params=pltpu.CompilerParams(
            collective_id=0, has_side_effects=True, vmem_limit_bytes=56 * 1024 * 1024
        ),
        name="beacon_backward",
    )(
        window, queries[0], raw_keys[0], raw_values[0], upstream[0], bkv, bqg,
        key_gain.reshape(heads, DH),
    )
    return tuple(out[None] for out in outs[:6]) + (outs[6].reshape(hd),)


def solution(mesh):
    slabs = P("dp", "ctx", None)
    return jax.shard_map(
        on_device,
        mesh=mesh,
        in_specs=(slabs,) * 8 + (P(), P("dp")),
        out_specs=(slabs,) * 6 + (P(),),
        check_vma=False,
    )
```

```python
from functools import partial
import math

import jax
import jax.numpy as jnp
from jax import lax
from jax.experimental import pallas as pl
from jax.experimental.pallas import tpu as pltpu
from jax.sharding import PartitionSpec as P

DH = 128
NY = 4
HALF = 128
ROWS = 144
AHEAD = 2
LAST = 3
WCOLS = 384
MESH = pl.DeviceIdType.MESH
NEG = -1e30
CONTRACT_LAST = (((1,), (1,)), ((), ()))
CONTRACT_FIRST = (((0,), (0,)), ((), ()))


def dot_t(a, b):
    return lax.dot_general(a, b, CONTRACT_LAST, preferred_element_type=jnp.float32)


def dot_f(a, b):
    return lax.dot_general(a, b, CONTRACT_FIRST, preferred_element_type=jnp.float32)


def dot_n(a, b):
    return jnp.dot(a, b, preferred_element_type=jnp.float32)


def kernel(
    ndp, nctx, heads, window,
    q_hbm, k_hbm, v_hbm, g_hbm, bq, bk, bv, bg, gain,
    dq_out, dk_out, dv_out, dbq, dbk, dbv, gain_out,
    q_s, k_s, v_s, g_s, kv_prev, pg_s, pg_r, own_s, bkv, bqg, stage,
    gath, kf, vf, bias_w, bias_b, rs_s, rs_r, zsum, ry_s, ry_r,
    gl, gd_r, gz_s, gz_r, gy_s, gy_r,
    in_sem, kv_send, kv_recv, gath_send, gathy_recv, gathz_send, gathz_recv,
    pg_send, pg_recv, rs_send, rs_recv, ry_send, ry_recv,
    gd_send, gd_recv, gz_send, gz_recv, gy_send, gy_recv,
):
    nz = nctx // NY
    nb = 2 * nctx
    groups = heads // 4
    scale = DH ** (-0.5)
    dp = lax.axis_index("dp")
    ctx = lax.axis_index("ctx")
    z = ctx // NY
    y = ctx % NY
    after = (ctx + 1) % nctx
    before = (ctx + nctx - 1) % nctx

    def zpeer(j):
        return ((z + j) % nz) * NY + y

    def ypeer(j):
        return z * NY + (y + j) % NY

    def remote(src, dst, send, recv, to):
        return pltpu.make_async_remote_copy(
            src_ref=src, dst_ref=dst, send_sem=send, recv_sem=recv,
            device_id=to, device_id_type=MESH,
        )

    def drain(ref, sem):
        pltpu.make_async_copy(ref, ref, sem).wait()

    loads = [
        pltpu.make_async_copy(src, dst, in_sem.at[i])
        for i, (src, dst) in enumerate(
            ((q_hbm, q_s), (k_hbm, k_s), (v_hbm, v_s), (g_hbm, g_s))
        )
    ]
    for load in loads:
        load.start()
    for i, source in enumerate((bk, bv, bq, bg)):
        wide = source[...].astype(jnp.float32)
        for h in range(heads):
            for k in range(2):
                piece = wide[k : k + 1, h * DH : (h + 1) * DH]
                if i < 2:
                    at = i * 8 + k * 4 + h % 4
                    stage[h // 4, at : at + 1] = piece
                else:
                    bqg[(i - 2) * 2 + k, h : h + 1] = piece
    bkv[...] = stage[...].astype(jnp.bfloat16)
    own_block = pltpu.make_async_copy(bkv, gath.at[:, ctx], in_sem.at[4])
    own_block.start()

    barrier = pltpu.get_barrier_semaphore()
    pl.semaphore_signal(barrier, inc=1, device_id=(dp, after), device_id_type=MESH)
    pl.semaphore_signal(barrier, inc=1, device_id=(dp, before), device_id_type=MESH)

    @pl.loop(1, NY)
    def _(j):
        pl.semaphore_signal(barrier, inc=1, device_id=(dp, ypeer(j)), device_id_type=MESH)

    @pl.loop(1, nz)
    def _(j):
        pl.semaphore_signal(barrier, inc=1, device_id=(dp, zpeer(j)), device_id_type=MESH)

    @pl.loop(1, ndp)
    def _(j):
        pl.semaphore_signal(
            barrier, inc=1, device_id=((dp + j) % ndp, ctx), device_id_type=MESH
        )

    pl.semaphore_wait(barrier, 2 + NY - 1 + nz - 1 + ndp - 1)

    @pl.loop(1, NY)
    def _(j):
        remote(
            bkv, gath.at[:, ctx], gath_send.at[0], gathy_recv.at[0], (dp, ypeer(j))
        ).start()

    def send_kv(h):
        cols = pl.ds(pl.multiple_of(h * DH, DH), DH)
        for i, source in enumerate((k_hbm, v_hbm)):
            remote(
                source.at[:, cols], kv_prev.at[h, i], kv_send.at[0], kv_recv.at[h],
                (dp, after),
            ).start()

    @pl.loop(0, AHEAD)
    def _(h):
        send_kv(h)

    width = window[0]
    for k in range(2):
        row = lax.broadcasted_iota(jnp.int32, (ROWS, WCOLS), 0)
        col = lax.broadcasted_iota(jnp.int32, (ROWS, WCOLS), 1)
        key_position = (ctx - 1) * 2 * HALF + HALF * k + col
        raw = (
            (row < HALF)
            & (col <= 2 * HALF + row)
            & (col > 2 * HALF + row - width)
            & (key_position >= 0)
        )
        beacon = (row == HALF) & (col >= 2 * HALF)
        bias_w[k] = jnp.where(raw | beacon, 0.0, NEG)
        row = lax.broadcasted_iota(jnp.int32, (ROWS, nb), 0)
        col = lax.broadcasted_iota(jnp.int32, (ROWS, nb), 1)
        position = ctx * 2 * HALF + HALF * k + row
        raw = (row < HALF) & (HALF * (col + 1) <= position - width + 1)
        beacon = (row == HALF) & (col <= 2 * ctx + k)
        bias_b[k] = jnp.where(raw | beacon, 0.0, NEG)

    drain(gath.at[:, pl.ds(0, NY - 1)], gathy_recv.at[0])
    own_block.wait()

    def spread(g):
        @pl.loop(z + 1, nz)
        def _(t):
            mine = pl.ds(z * NY, NY)
            remote(
                gath.at[g, mine], gath.at[g, mine], gathz_send.at[t], gathz_recv.at[g, z],
                (dp, t * NY + y),
            ).start()

    spread(0)

    @pl.loop(z + 1, nz)
    def _(t):
        gath[:, pl.ds(t * NY, NY)] = jnp.zeros((groups, NY, 16, DH), jnp.bfloat16)

    @pl.loop(0, z)
    def _(t):
        rs_r[:, t] = jnp.zeros((heads, 16, DH), jnp.bfloat16)


    for load in loads:
        load.wait()

    first_row = lax.broadcasted_iota(jnp.int32, (16, DH), 0) == 0
    fold = scale * math.log2(math.e)

    @pl.loop(0, groups)
    def _(g):
        @pl.loop(0, z)
        def _(t):
            drain(gath.at[g, pl.ds(t * NY, NY)], gathz_recv.at[g, t])

        @pl.when(g + 1 < groups)
        def _():
            spread(g + 1)

        block = gath[g].astype(jnp.float32)
        kf[...] = block[:, 0:8].reshape(nctx * 8, DH)
        vf[...] = block[:, 8:16].reshape(nctx * 8, DH)

        @pl.loop(0, 4)
        def _(hl):
            h = g * 4 + hl
            cols = pl.ds(pl.multiple_of(h * DH, DH), DH)
            raw_b = kf[pl.ds(hl, nb, stride=4), :]
            gained = (raw_b * gain[pl.ds(h, 1), :]).astype(jnp.bfloat16)
            value_b = vf[pl.ds(hl, nb, stride=4), :].astype(jnp.bfloat16)
            drain(kv_prev.at[h], kv_recv.at[h])

            @pl.when(h + AHEAD < heads)
            def _():
                send_kv(h + AHEAD)

            win_k = []
            win_v = []
            for k in range(2):
                win_k.append(
                    jnp.concatenate(
                        [kv_prev[h, 0, HALF * k :], k_s[0 : HALF * (k + 1), cols]], axis=0
                    )
                )
                win_v.append(
                    jnp.concatenate(
                        [kv_prev[h, 1, HALF * k :], v_s[0 : HALF * (k + 1), cols]], axis=0
                    )
                )
            dk_w, dv_w, dk_b, dv_b = [], [], [], []
            for k in range(2):
                extra_q = jnp.where(first_row, bqg[k, pl.ds(h, 1), :], 0.0)
                extra_g = jnp.where(first_row, bqg[2 + k, pl.ds(h, 1), :], 0.0)
                rows = slice(HALF * k, HALF * (k + 1))
                q = jnp.concatenate([q_s[rows, cols], extra_q.astype(jnp.bfloat16)], axis=0)
                up = jnp.concatenate([g_s[rows, cols], extra_g.astype(jnp.bfloat16)], axis=0)
                s_w = dot_t(q, win_k[k]) * fold + bias_w[k]
                s_b = dot_t(q, gained) * fold + bias_b[k]
                peak = jnp.maximum(
                    jnp.max(s_w, axis=1, keepdims=True), jnp.max(s_b, axis=1, keepdims=True)
                )
                e_w = jnp.exp2(s_w - peak)
                e_b = jnp.exp2(s_b - peak)
                total = jnp.sum(e_w, axis=1, keepdims=True) + jnp.sum(
                    e_b, axis=1, keepdims=True
                )
                inverse = 1.0 / total
                p_w = e_w * inverse
                p_b = e_b * inverse
                low_w = p_w.astype(jnp.bfloat16)
                low_b = p_b.astype(jnp.bfloat16)
                dp_w = dot_t(up, win_v[k])
                dp_b = dot_t(up, value_b)
                delta = jnp.sum(
                    low_w.astype(jnp.float32) * dp_w, axis=1, keepdims=True
                ) + jnp.sum(low_b.astype(jnp.float32) * dp_b, axis=1, keepdims=True)
                ds_w = (p_w * (dp_w - delta)).astype(jnp.bfloat16)
                ds_b = (p_b * (dp_b - delta)).astype(jnp.bfloat16)
                dk_w.append(dot_f(ds_w, q))
                dv_w.append(dot_f(low_w, up))
                dk_b.append(dot_f(ds_b, q))
                dv_b.append(dot_f(low_b, up))
                dq = (dot_n(ds_w, win_k[k]) + dot_n(ds_b, gained)) * scale
                dq_out[rows, cols] = dq[0:HALF].astype(jnp.bfloat16)
                gz_s[1 + k, pl.ds(h, 1), :] = dq[HALF : HALF + 1]
            for i, (t, c) in enumerate(((dk_w, scale), (dv_w, 1.0))):
                pg_s[h, i, 0:HALF] = (t[0][0:HALF] * c).astype(jnp.bfloat16)
                pg_s[h, i, HALF:] = (
                    (t[0][HALF : 2 * HALF] + t[1][0:HALF]) * c
                ).astype(jnp.bfloat16)
            part_k = (dk_b[0] + dk_b[1]) * scale
            part_v = dv_b[0] + dv_b[1]
            rs_s[h] = jnp.concatenate(
                [part_k.reshape(nz, 8, DH), part_v.reshape(nz, 8, DH)], axis=1
            ).astype(jnp.bfloat16)
            gl[pl.ds(h, 1), :] = jnp.sum(raw_b * part_k, axis=0, keepdims=True)
            for i, (t, c) in enumerate(((dk_w, scale), (dv_w, 1.0))):
                own_s[h, i, 0:HALF] = (t[0][2 * HALF :] + t[1][HALF : 2 * HALF]) * c
                own_s[h, i, HALF:] = t[1][2 * HALF :] * c
            remote(
                pg_s.at[h], pg_r.at[h], pg_send.at[0], pg_recv.at[h], (dp, before)
            ).start()

            @pl.loop(0, z)
            def _(t):
                remote(
                    rs_s.at[h, t], rs_r.at[h, z], rs_send.at[t], rs_recv.at[z],
                    (dp, t * NY + y),
                ).start()

    @pl.loop(1, ndp)
    def _(j):
        remote(
            gl, gd_r.at[dp], gd_send.at[0], gd_recv.at[0], ((dp + j) % ndp, ctx)
        ).start()

    gd_r[dp] = gl[...]
    rs_r[:, z] = rs_s[:, z]

    drain(gd_r.at[pl.ds(0, ndp - 1)], gd_recv.at[0])
    gz_s[0] = jnp.sum(gd_r[...], axis=0)
    gz_r[z] = gz_s[0]

    @pl.loop(1, nz)
    def _(j):
        remote(
            gz_s.at[0], gz_r.at[z], gz_send.at[0], gz_recv.at[0], (dp, zpeer(j))
        ).start()

    @pl.loop(z + 1, nz)
    def _(t):
        drain(rs_r.at[:, t], rs_recv.at[t])

    zsum[...] = jnp.sum(rs_r[...].astype(jnp.float32), axis=1).reshape(heads * 16, DH)
    for t in range(NY):
        for kv in range(2):
            for k in range(2):
                ry_s[t, 2 * kv + k] = zsum[
                    pl.ds(kv * 8 + 2 * t + k, heads, stride=16), :
                ].astype(jnp.bfloat16)

    @pl.loop(1, NY)
    def _(j):
        remote(
            ry_s.at[(y + j) % NY], ry_r.at[y], ry_send.at[0], ry_recv.at[0], (dp, ypeer(j))
        ).start()

    ry_r[y] = ry_s[y]

    def finish(h):
        cols = pl.ds(pl.multiple_of(h * DH, DH), DH)
        drain(pg_r.at[h], pg_recv.at[h])
        total = own_s[h] + pg_r[h].astype(jnp.float32)
        dk_out[:, cols] = total[0].astype(jnp.bfloat16)
        dv_out[:, cols] = total[1].astype(jnp.bfloat16)

    @pl.loop(0, heads - LAST)
    def _(h):
        finish(h)

    drain(gz_r.at[pl.ds(0, nz - 1)], gz_recv.at[0])
    gy_s[...] = jnp.sum(gz_r[...], axis=0)
    gy_r[y] = gy_s[...]

    @pl.loop(1, NY)
    def _(j):
        remote(gy_s, gy_r.at[y], gy_send.at[0], gy_recv.at[0], (dp, ypeer(j))).start()

    @pl.loop(heads - LAST, heads)
    def _(h):
        finish(h)

    drain(ry_r.at[pl.ds(0, NY - 1)], ry_recv.at[0])
    own = jnp.sum(ry_r[...].astype(jnp.float32), axis=0)
    for h in range(heads):
        cols = slice(h * DH, (h + 1) * DH)
        scaled = gain[h : h + 1]
        rows_q = [gz_s[1 + k, h : h + 1] for k in range(2)]
        rows_k = [own[k, h : h + 1] * scaled for k in range(2)]
        rows_v = [own[2 + k, h : h + 1] for k in range(2)]
        dbq[:, cols] = jnp.concatenate(rows_q, axis=0).astype(jnp.bfloat16)
        dbk[:, cols] = jnp.concatenate(rows_k, axis=0).astype(jnp.bfloat16)
        dbv[:, cols] = jnp.concatenate(rows_v, axis=0).astype(jnp.bfloat16)
    drain(gy_r.at[pl.ds(0, NY - 1)], gy_recv.at[0])
    gain_out[...] = jnp.sum(gy_r[...], axis=0)

    drain(gath.at[:, pl.ds(0, NY - 1)], gath_send.at[0])

    @pl.loop(z + 1, nz)
    def _(t):
        drain(gath.at[:, pl.ds(0, NY)], gathz_send.at[t])

    drain(kv_prev, kv_send.at[0])
    drain(pg_s, pg_send.at[0])

    @pl.loop(0, z)
    def _(t):
        drain(rs_s.at[:, t], rs_send.at[t])

    drain(ry_s.at[pl.ds(0, NY - 1)], ry_send.at[0])
    drain(gd_r.at[pl.ds(0, ndp - 1)], gd_send.at[0])
    drain(gz_r.at[pl.ds(0, nz - 1)], gz_send.at[0])
    drain(gy_r.at[pl.ds(0, NY - 1)], gy_send.at[0])


def write_out(*refs):
    sems = refs[14]
    copies = [
        pltpu.make_async_copy(refs[i], refs[7 + i], sems.at[i]) for i in range(7)
    ]
    for copy in copies:
        copy.start()
    for copy in copies:
        copy.wait()


def on_device(
    queries, raw_keys, raw_values, beacon_queries, beacon_keys, beacon_values,
    upstream, beacon_upstream, key_gain, window,
):
    ndp = lax.axis_size("dp")
    nctx = lax.axis_size("ctx")
    nz = nctx // NY
    nb = 2 * nctx
    slab = queries.shape[1]
    hd = queries.shape[2]
    heads = hd // DH
    groups = heads // 4
    bf16, f32 = jnp.bfloat16, jnp.float32

    vmem = pl.BlockSpec(memory_space=pltpu.VMEM)
    anyspace = pl.BlockSpec(memory_space=pl.ANY)
    dma = pltpu.SemaphoreType.DMA
    few = pltpu.VMEM((2, hd), bf16)
    big = pltpu.VMEM((slab, hd), bf16)
    outs = pl.pallas_call(
        partial(kernel, ndp, nctx, heads),
        out_shape=(
            big, big, big, few, few, few, pltpu.VMEM((heads, DH), f32),
        ),
        in_specs=[pl.BlockSpec(memory_space=pltpu.SMEM)] + [anyspace] * 4 + [vmem] * 5,
        out_specs=(vmem,) * 7,
        scratch_shapes=[
            pltpu.VMEM((slab, hd), bf16),
            pltpu.VMEM((slab, hd), bf16),
            pltpu.VMEM((slab, hd), bf16),
            pltpu.VMEM((slab, hd), bf16),
            pltpu.VMEM((heads, 2, slab, DH), bf16),
            pltpu.VMEM((heads, 2, slab, DH), bf16),
            pltpu.VMEM((heads, 2, slab, DH), bf16),
            pltpu.VMEM((heads, 2, slab, DH), f32),
            pltpu.VMEM((groups, 16, DH), bf16),
            pltpu.VMEM((4, heads, DH), f32),
            pltpu.VMEM((groups, 16, DH), f32),
            pltpu.VMEM((groups, nctx, 16, DH), bf16),
            pltpu.VMEM((nctx * 8, DH), f32),
            pltpu.VMEM((nctx * 8, DH), f32),
            pltpu.VMEM((2, ROWS, WCOLS), f32),
            pltpu.VMEM((2, ROWS, nb), f32),
            pltpu.VMEM((heads, nz, 16, DH), bf16),
            pltpu.VMEM((heads, nz, 16, DH), bf16),
            pltpu.VMEM((heads * 16, DH), f32),
            pltpu.VMEM((NY, 4, heads, DH), bf16),
            pltpu.VMEM((NY, 4, heads, DH), bf16),
            pltpu.VMEM((heads, DH), f32),
            pltpu.VMEM((ndp, heads, DH), f32),
            pltpu.VMEM((3, heads, DH), f32),
            pltpu.VMEM((nz, heads, DH), f32),
            pltpu.VMEM((heads, DH), f32),
            pltpu.VMEM((NY, heads, DH), f32),
            dma((5,)), dma((1,)), dma((heads,)), dma((1,)), dma((1,)),
            dma((nz,)), dma((groups, nz)), dma((1,)), dma((heads,)),
            dma((nz,)), dma((nz,)), dma((1,)), dma((1,)),
            dma((1,)), dma((1,)), dma((1,)), dma((1,)), dma((1,)), dma((1,)),
        ],
        compiler_params=pltpu.CompilerParams(
            collective_id=0, has_side_effects=True, vmem_limit_bytes=56 * 1024 * 1024
        ),
        name="beacon_backward",
    )(
        window, queries[0], raw_keys[0], raw_values[0], upstream[0],
        beacon_queries[0], beacon_keys[0], beacon_values[0], beacon_upstream[0],
        key_gain.reshape(heads, DH),
    )
    plain = [jax.ShapeDtypeStruct(out.shape, out.dtype) for out in outs]
    outs = pl.pallas_call(
        write_out,
        out_shape=plain,
        in_specs=[anyspace] * 7,
        out_specs=[anyspace] * 7,
        scratch_shapes=[dma((7,))],
        name="write_out",
    )(*[pltpu.with_memory_space_constraint(out, pltpu.VMEM) for out in outs])
    return tuple(out[None] for out in outs[:6]) + (outs[6].reshape(hd),)


def solution(mesh):
    slabs = P("dp", "ctx", None)
    return jax.shard_map(
        on_device,
        mesh=mesh,
        in_specs=(slabs,) * 8 + (P(), P("dp")),
        out_specs=(slabs,) * 6 + (P(),),
        check_vma=False,
    )
```

```python
from functools import partial
import math

import jax
import jax.numpy as jnp
from jax import lax
from jax.experimental import pallas as pl
from jax.experimental.pallas import tpu as pltpu
from jax.sharding import PartitionSpec as P

DH = 128
NY = 4
HALF = 128
ROWS = 144
AHEAD = 4
LAST = 3
WCOLS = 384
MESH = pl.DeviceIdType.MESH
NEG = -1e30
CONTRACT_LAST = (((1,), (1,)), ((), ()))
CONTRACT_FIRST = (((0,), (0,)), ((), ()))


def dot_t(a, b):
    return lax.dot_general(a, b, CONTRACT_LAST, preferred_element_type=jnp.float32)


def dot_f(a, b):
    return lax.dot_general(a, b, CONTRACT_FIRST, preferred_element_type=jnp.float32)


def dot_n(a, b):
    return jnp.dot(a, b, preferred_element_type=jnp.float32)


def kernel(
    ndp, nctx, heads, window,
    q_hbm, k_hbm, v_hbm, g_hbm, bq, bk, bv, bg, gain,
    dq_out, dk_out, dv_out, dbq, dbk, dbv, gain_out,
    q_s, k_s, v_s, g_s, kv_prev, pg_s, pg_r, own_s, bkv, bqg, stage,
    gath, kf, vf, bias_w, bias_b, rs_s, rs_r, zsum, ry_s, ry_r,
    gl, gd_r, gz_s, gz_r, gy_s, gy_r,
    in_sem, kv_send, kv_recv, gath_send, gathy_recv, gathz_send, gathz_recv,
    pg_send, pg_recv, rs_send, rs_recv, ry_send, ry_recv,
    gd_send, gd_recv, gz_send, gz_recv, gy_send, gy_recv,
):
    nz = nctx // NY
    nb = 2 * nctx
    groups = heads // 4
    scale = DH ** (-0.5)
    dp = lax.axis_index("dp")
    ctx = lax.axis_index("ctx")
    z = ctx // NY
    y = ctx % NY
    after = (ctx + 1) % nctx
    before = (ctx + nctx - 1) % nctx

    def zpeer(j):
        return ((z + j) % nz) * NY + y

    def ypeer(j):
        return z * NY + (y + j) % NY

    def remote(src, dst, send, recv, to):
        return pltpu.make_async_remote_copy(
            src_ref=src, dst_ref=dst, send_sem=send, recv_sem=recv,
            device_id=to, device_id_type=MESH,
        )

    def drain(ref, sem):
        pltpu.make_async_copy(ref, ref, sem).wait()

    loads = [
        pltpu.make_async_copy(src, dst, in_sem.at[i])
        for i, (src, dst) in enumerate(
            ((q_hbm, q_s), (k_hbm, k_s), (v_hbm, v_s), (g_hbm, g_s))
        )
    ]
    for load in loads:
        load.start()
    for i, source in enumerate((bk, bv, bq, bg)):
        wide = source[...].astype(jnp.float32)
        for h in range(heads):
            for k in range(2):
                piece = wide[k : k + 1, h * DH : (h + 1) * DH]
                if i < 2:
                    at = i * 8 + k * 4 + h % 4
                    stage[h // 4, at : at + 1] = piece
                else:
                    bqg[(i - 2) * 2 + k, h : h + 1] = piece
    bkv[...] = stage[...].astype(jnp.bfloat16)
    own_block = pltpu.make_async_copy(bkv, gath.at[:, ctx], in_sem.at[4])
    own_block.start()

    barrier = pltpu.get_barrier_semaphore()
    pl.semaphore_signal(barrier, inc=1, device_id=(dp, after), device_id_type=MESH)
    pl.semaphore_signal(barrier, inc=1, device_id=(dp, before), device_id_type=MESH)

    @pl.loop(1, NY)
    def _(j):
        pl.semaphore_signal(barrier, inc=1, device_id=(dp, ypeer(j)), device_id_type=MESH)

    @pl.loop(1, nz)
    def _(j):
        pl.semaphore_signal(barrier, inc=1, device_id=(dp, zpeer(j)), device_id_type=MESH)

    @pl.loop(1, ndp)
    def _(j):
        pl.semaphore_signal(
            barrier, inc=1, device_id=((dp + j) % ndp, ctx), device_id_type=MESH
        )

    pl.semaphore_wait(barrier, 2 + NY - 1 + nz - 1 + ndp - 1)

    @pl.loop(1, NY)
    def _(j):
        remote(
            bkv, gath.at[:, ctx], gath_send.at[0], gathy_recv.at[0], (dp, ypeer(j))
        ).start()

    def send_kv(h):
        cols = pl.ds(pl.multiple_of(h * DH, DH), DH)
        for i, source in enumerate((k_hbm, v_hbm)):
            remote(
                source.at[:, cols], kv_prev.at[h, i], kv_send.at[0], kv_recv.at[h],
                (dp, after),
            ).start()

    @pl.loop(0, AHEAD)
    def _(h):
        send_kv(h)

    width = window[0]
    for k in range(2):
        row = lax.broadcasted_iota(jnp.int32, (ROWS, WCOLS), 0)
        col = lax.broadcasted_iota(jnp.int32, (ROWS, WCOLS), 1)
        key_position = (ctx - 1) * 2 * HALF + HALF * k + col
        raw = (
            (row < HALF)
            & (col <= 2 * HALF + row)
            & (col > 2 * HALF + row - width)
            & (key_position >= 0)
        )
        beacon = (row == HALF) & (col >= 2 * HALF)
        bias_w[k] = jnp.where(raw | beacon, 0.0, NEG)
        row = lax.broadcasted_iota(jnp.int32, (ROWS, nb), 0)
        col = lax.broadcasted_iota(jnp.int32, (ROWS, nb), 1)
        position = ctx * 2 * HALF + HALF * k + row
        raw = (row < HALF) & (HALF * (col + 1) <= position - width + 1)
        beacon = (row == HALF) & (col <= 2 * ctx + k)
        bias_b[k] = jnp.where(raw | beacon, 0.0, NEG)

    drain(gath.at[:, pl.ds(0, NY - 1)], gathy_recv.at[0])
    own_block.wait()

    def spread(g):
        @pl.loop(z + 1, nz)
        def _(t):
            mine = pl.ds(z * NY, NY)
            remote(
                gath.at[g, mine], gath.at[g, mine], gathz_send.at[t], gathz_recv.at[g, z],
                (dp, t * NY + y),
            ).start()

    spread(0)

    @pl.loop(z + 1, nz)
    def _(t):
        gath[:, pl.ds(t * NY, NY)] = jnp.zeros((groups, NY, 16, DH), jnp.bfloat16)

    @pl.loop(0, z)
    def _(t):
        rs_r[:, t] = jnp.zeros((heads, 16, DH), jnp.bfloat16)


    for load in loads:
        load.wait()

    first_row = lax.broadcasted_iota(jnp.int32, (16, DH), 0) == 0
    fold = scale * math.log2(math.e)

    @pl.loop(0, groups)
    def _(g):
        @pl.loop(0, z)
        def _(t):
            drain(gath.at[g, pl.ds(t * NY, NY)], gathz_recv.at[g, t])

        @pl.when(g + 1 < groups)
        def _():
            spread(g + 1)

        block = gath[g].astype(jnp.float32)
        kf[...] = block[:, 0:8].reshape(nctx * 8, DH)
        vf[...] = block[:, 8:16].reshape(nctx * 8, DH)

        @pl.loop(0, 4)
        def _(hl):
            h = g * 4 + hl
            cols = pl.ds(pl.multiple_of(h * DH, DH), DH)
            raw_b = kf[pl.ds(hl, nb, stride=4), :]
            gained = (raw_b * gain[pl.ds(h, 1), :]).astype(jnp.bfloat16)
            value_b = vf[pl.ds(hl, nb, stride=4), :].astype(jnp.bfloat16)
            drain(kv_prev.at[h], kv_recv.at[h])

            @pl.when(h + AHEAD < heads)
            def _():
                send_kv(h + AHEAD)

            win_k = []
            win_v = []
            for k in range(2):
                win_k.append(
                    jnp.concatenate(
                        [kv_prev[h, 0, HALF * k :], k_s[0 : HALF * (k + 1), cols]], axis=0
                    )
                )
                win_v.append(
                    jnp.concatenate(
                        [kv_prev[h, 1, HALF * k :], v_s[0 : HALF * (k + 1), cols]], axis=0
                    )
                )
            dk_w, dv_w, dk_b, dv_b = [], [], [], []
            for k in range(2):
                extra_q = jnp.where(first_row, bqg[k, pl.ds(h, 1), :], 0.0)
                extra_g = jnp.where(first_row, bqg[2 + k, pl.ds(h, 1), :], 0.0)
                rows = slice(HALF * k, HALF * (k + 1))
                q = jnp.concatenate([q_s[rows, cols], extra_q.astype(jnp.bfloat16)], axis=0)
                up = jnp.concatenate([g_s[rows, cols], extra_g.astype(jnp.bfloat16)], axis=0)
                s_w = dot_t(q, win_k[k]) * fold + bias_w[k]
                s_b = dot_t(q, gained) * fold + bias_b[k]
                peak = jnp.maximum(
                    jnp.max(s_w, axis=1, keepdims=True), jnp.max(s_b, axis=1, keepdims=True)
                )
                e_w = jnp.exp2(s_w - peak)
                e_b = jnp.exp2(s_b - peak)
                total = jnp.sum(e_w, axis=1, keepdims=True) + jnp.sum(
                    e_b, axis=1, keepdims=True
                )
                inverse = 1.0 / total
                p_w = e_w * inverse
                p_b = e_b * inverse
                low_w = p_w.astype(jnp.bfloat16)
                low_b = p_b.astype(jnp.bfloat16)
                dp_w = dot_t(up, win_v[k])
                dp_b = dot_t(up, value_b)
                delta = jnp.sum(
                    low_w.astype(jnp.float32) * dp_w, axis=1, keepdims=True
                ) + jnp.sum(low_b.astype(jnp.float32) * dp_b, axis=1, keepdims=True)
                ds_w = (p_w * (dp_w - delta)).astype(jnp.bfloat16)
                ds_b = (p_b * (dp_b - delta)).astype(jnp.bfloat16)
                dk_w.append(dot_f(ds_w, q))
                dv_w.append(dot_f(low_w, up))
                dk_b.append(dot_f(ds_b, q))
                dv_b.append(dot_f(low_b, up))
                dq = (dot_n(ds_w, win_k[k]) + dot_n(ds_b, gained)) * scale
                dq_out[rows, cols] = dq[0:HALF].astype(jnp.bfloat16)
                gz_s[1 + k, pl.ds(h, 1), :] = dq[HALF : HALF + 1]
            for i, (t, c) in enumerate(((dk_w, scale), (dv_w, 1.0))):
                pg_s[h, i, 0:HALF] = (t[0][0:HALF] * c).astype(jnp.bfloat16)
                pg_s[h, i, HALF:] = (
                    (t[0][HALF : 2 * HALF] + t[1][0:HALF]) * c
                ).astype(jnp.bfloat16)
            part_k = (dk_b[0] + dk_b[1]) * scale
            part_v = dv_b[0] + dv_b[1]
            rs_s[h] = jnp.concatenate(
                [part_k.reshape(nz, 8, DH), part_v.reshape(nz, 8, DH)], axis=1
            ).astype(jnp.bfloat16)
            gl[pl.ds(h, 1), :] = jnp.sum(raw_b * part_k, axis=0, keepdims=True)
            for i, (t, c) in enumerate(((dk_w, scale), (dv_w, 1.0))):
                own_s[h, i, 0:HALF] = (t[0][2 * HALF :] + t[1][HALF : 2 * HALF]) * c
                own_s[h, i, HALF:] = t[1][2 * HALF :] * c
            remote(
                pg_s.at[h], pg_r.at[h], pg_send.at[0], pg_recv.at[h], (dp, before)
            ).start()

            @pl.loop(0, z)
            def _(t):
                remote(
                    rs_s.at[h, t], rs_r.at[h, z], rs_send.at[t], rs_recv.at[z],
                    (dp, t * NY + y),
                ).start()

    @pl.loop(1, ndp)
    def _(j):
        remote(
            gl, gd_r.at[dp], gd_send.at[0], gd_recv.at[0], ((dp + j) % ndp, ctx)
        ).start()

    gd_r[dp] = gl[...]
    rs_r[:, z] = rs_s[:, z]

    drain(gd_r.at[pl.ds(0, ndp - 1)], gd_recv.at[0])
    gz_s[0] = jnp.sum(gd_r[...], axis=0)
    gz_r[z] = gz_s[0]

    @pl.loop(1, nz)
    def _(j):
        remote(
            gz_s.at[0], gz_r.at[z], gz_send.at[0], gz_recv.at[0], (dp, zpeer(j))
        ).start()

    @pl.loop(z + 1, nz)
    def _(t):
        drain(rs_r.at[:, t], rs_recv.at[t])

    zsum[...] = jnp.sum(rs_r[...].astype(jnp.float32), axis=1).reshape(heads * 16, DH)
    for t in range(NY):
        for kv in range(2):
            for k in range(2):
                ry_s[t, 2 * kv + k] = zsum[
                    pl.ds(kv * 8 + 2 * t + k, heads, stride=16), :
                ].astype(jnp.bfloat16)

    @pl.loop(1, NY)
    def _(j):
        remote(
            ry_s.at[(y + j) % NY], ry_r.at[y], ry_send.at[0], ry_recv.at[0], (dp, ypeer(j))
        ).start()

    ry_r[y] = ry_s[y]

    def finish(h):
        cols = pl.ds(pl.multiple_of(h * DH, DH), DH)
        drain(pg_r.at[h], pg_recv.at[h])
        total = own_s[h] + pg_r[h].astype(jnp.float32)
        dk_out[:, cols] = total[0].astype(jnp.bfloat16)
        dv_out[:, cols] = total[1].astype(jnp.bfloat16)

    @pl.loop(0, heads - LAST)
    def _(h):
        finish(h)

    drain(gz_r.at[pl.ds(0, nz - 1)], gz_recv.at[0])
    gy_s[...] = jnp.sum(gz_r[...], axis=0)
    gy_r[y] = gy_s[...]

    @pl.loop(1, NY)
    def _(j):
        remote(gy_s, gy_r.at[y], gy_send.at[0], gy_recv.at[0], (dp, ypeer(j))).start()

    @pl.loop(heads - LAST, heads)
    def _(h):
        finish(h)

    drain(ry_r.at[pl.ds(0, NY - 1)], ry_recv.at[0])
    own = jnp.sum(ry_r[...].astype(jnp.float32), axis=0)
    for h in range(heads):
        cols = slice(h * DH, (h + 1) * DH)
        scaled = gain[h : h + 1]
        rows_q = [gz_s[1 + k, h : h + 1] for k in range(2)]
        rows_k = [own[k, h : h + 1] * scaled for k in range(2)]
        rows_v = [own[2 + k, h : h + 1] for k in range(2)]
        dbq[:, cols] = jnp.concatenate(rows_q, axis=0).astype(jnp.bfloat16)
        dbk[:, cols] = jnp.concatenate(rows_k, axis=0).astype(jnp.bfloat16)
        dbv[:, cols] = jnp.concatenate(rows_v, axis=0).astype(jnp.bfloat16)
    drain(gy_r.at[pl.ds(0, NY - 1)], gy_recv.at[0])
    gain_out[...] = jnp.sum(gy_r[...], axis=0)

    drain(gath.at[:, pl.ds(0, NY - 1)], gath_send.at[0])

    @pl.loop(z + 1, nz)
    def _(t):
        drain(gath.at[:, pl.ds(0, NY)], gathz_send.at[t])

    drain(kv_prev, kv_send.at[0])
    drain(pg_s, pg_send.at[0])

    @pl.loop(0, z)
    def _(t):
        drain(rs_s.at[:, t], rs_send.at[t])

    drain(ry_s.at[pl.ds(0, NY - 1)], ry_send.at[0])
    drain(gd_r.at[pl.ds(0, ndp - 1)], gd_send.at[0])
    drain(gz_r.at[pl.ds(0, nz - 1)], gz_send.at[0])
    drain(gy_r.at[pl.ds(0, NY - 1)], gy_send.at[0])


def write_out(*refs):
    sems = refs[14]
    copies = [
        pltpu.make_async_copy(refs[i], refs[7 + i], sems.at[i]) for i in range(7)
    ]
    for copy in copies:
        copy.start()
    for copy in copies:
        copy.wait()


def on_device(
    queries, raw_keys, raw_values, beacon_queries, beacon_keys, beacon_values,
    upstream, beacon_upstream, key_gain, window,
):
    ndp = lax.axis_size("dp")
    nctx = lax.axis_size("ctx")
    nz = nctx // NY
    nb = 2 * nctx
    slab = queries.shape[1]
    hd = queries.shape[2]
    heads = hd // DH
    groups = heads // 4
    bf16, f32 = jnp.bfloat16, jnp.float32

    vmem = pl.BlockSpec(memory_space=pltpu.VMEM)
    anyspace = pl.BlockSpec(memory_space=pl.ANY)
    dma = pltpu.SemaphoreType.DMA
    few = pltpu.VMEM((2, hd), bf16)
    big = pltpu.VMEM((slab, hd), bf16)
    outs = pl.pallas_call(
        partial(kernel, ndp, nctx, heads),
        out_shape=(
            big, big, big, few, few, few, pltpu.VMEM((heads, DH), f32),
        ),
        in_specs=[pl.BlockSpec(memory_space=pltpu.SMEM)] + [anyspace] * 4 + [vmem] * 5,
        out_specs=(vmem,) * 7,
        scratch_shapes=[
            pltpu.VMEM((slab, hd), bf16),
            pltpu.VMEM((slab, hd), bf16),
            pltpu.VMEM((slab, hd), bf16),
            pltpu.VMEM((slab, hd), bf16),
            pltpu.VMEM((heads, 2, slab, DH), bf16),
            pltpu.VMEM((heads, 2, slab, DH), bf16),
            pltpu.VMEM((heads, 2, slab, DH), bf16),
            pltpu.VMEM((heads, 2, slab, DH), f32),
            pltpu.VMEM((groups, 16, DH), bf16),
            pltpu.VMEM((4, heads, DH), f32),
            pltpu.VMEM((groups, 16, DH), f32),
            pltpu.VMEM((groups, nctx, 16, DH), bf16),
            pltpu.VMEM((nctx * 8, DH), f32),
            pltpu.VMEM((nctx * 8, DH), f32),
            pltpu.VMEM((2, ROWS, WCOLS), f32),
            pltpu.VMEM((2, ROWS, nb), f32),
            pltpu.VMEM((heads, nz, 16, DH), bf16),
            pltpu.VMEM((heads, nz, 16, DH), bf16),
            pltpu.VMEM((heads * 16, DH), f32),
            pltpu.VMEM((NY, 4, heads, DH), bf16),
            pltpu.VMEM((NY, 4, heads, DH), bf16),
            pltpu.VMEM((heads, DH), f32),
            pltpu.VMEM((ndp, heads, DH), f32),
            pltpu.VMEM((3, heads, DH), f32),
            pltpu.VMEM((nz, heads, DH), f32),
            pltpu.VMEM((heads, DH), f32),
            pltpu.VMEM((NY, heads, DH), f32),
            dma((5,)), dma((1,)), dma((heads,)), dma((1,)), dma((1,)),
            dma((nz,)), dma((groups, nz)), dma((1,)), dma((heads,)),
            dma((nz,)), dma((nz,)), dma((1,)), dma((1,)),
            dma((1,)), dma((1,)), dma((1,)), dma((1,)), dma((1,)), dma((1,)),
        ],
        compiler_params=pltpu.CompilerParams(
            collective_id=0, has_side_effects=True, vmem_limit_bytes=56 * 1024 * 1024
        ),
        name="beacon_backward",
    )(
        window, queries[0], raw_keys[0], raw_values[0], upstream[0],
        beacon_queries[0], beacon_keys[0], beacon_values[0], beacon_upstream[0],
        key_gain.reshape(heads, DH),
    )
    plain = [jax.ShapeDtypeStruct(out.shape, out.dtype) for out in outs]
    outs = pl.pallas_call(
        write_out,
        out_shape=plain,
        in_specs=[anyspace] * 7,
        out_specs=[anyspace] * 7,
        scratch_shapes=[dma((7,))],
        name="write_out",
    )(*[pltpu.with_memory_space_constraint(out, pltpu.VMEM) for out in outs])
    return tuple(out[None] for out in outs[:6]) + (outs[6].reshape(hd),)


def solution(mesh):
    slabs = P("dp", "ctx", None)
    return jax.shard_map(
        on_device,
        mesh=mesh,
        in_specs=(slabs,) * 8 + (P(), P("dp")),
        out_specs=(slabs,) * 6 + (P(),),
        check_vma=False,
    )
```
